32 devices in a mesh: lon: 8 (over z, x), lat: 4 (over y, core).
Axes of the slice: x: 2, y: 2, z: 4, core: 2. Of those that a mesh axis runs over, the one named last changes fastest.
Arguments:
- increment: bfloat16 [256, 512, 128], P('lon', 'lat'), may hold values from -6 to 6
- jacobian: bfloat16 [512, 128, 3072], P(('lon', 'lat')), may hold values from -0.0625 to 0.0625
- lat_weight: float32 [512, 8], P(('lon', 'lat')), may hold values from 0.2 to 2
- centre: int32 [512], P(('lon', 'lat')), may hold values from 0 to 31
- west: int32 [512], P(('lon', 'lat')), may hold values from 0 to 32
- east: int32 [512], P(('lon', 'lat')), may hold values from 0 to 32
- lat_offset: int32 [512], P(('lon', 'lat')), may hold values from 0 to 504
- lev_offset: int32 [512], P(('lon', 'lat')), may hold values from 0 to 96
Outputs:
- departures: float32 [512, 128], P(('lon', 'lat'))
The draws below stay inside these ranges and needn't reach their ends.
All inputs are finite; a program needn't handle non-finite values.
Results may differ from the reference program's by a relative error of at most 0.0029.
Values may be sent and summed in bfloat16 or wider, within the bound.
A program may use at most 128 MiB of HBM per device.

```python
import math
import jax
import jax.numpy as jnp
from jax import lax

LON_DEV = 32
SLOTS = 16
LEV = 128
NTAN = 128
BLAT = 8
BLEV = 32
LON = 256
LAT = 512
SCANS = 512
N_LON = 8
N_LAT = 4


def place_ends(entries, key, least, largest):
    dims = entries.shape
    spot = [jax.random.randint(jax.random.fold_in(key, axis), (), 0, dims[axis]) for axis in range(len(dims))]
    entries = entries.at[tuple(spot)].set(least)
    longest = dims.index(max(dims))
    spot[longest] = (spot[longest] + 1) % dims[longest]
    return entries.at[tuple(spot)].set(largest)


def level_of(own_key, dims, pieces, low, high):
    factor_of, own = 1.0, jax.random.fold_in(own_key, 6)
    for dim, shards_of in pieces:
        heights = jnp.exp(jax.random.uniform(jax.random.fold_in(own, dim), (shards_of,), jnp.float32, low / len(pieces), high / len(pieces)))
        factor_of = factor_of * jnp.repeat(heights, dims[dim] // shards_of).reshape([-1 if axis == dim else 1 for axis in range(len(dims))])
    return factor_of


def scatter_about(own_key, dims, deviation, bound, pieces=(), held_as=jnp.bfloat16):
    entries = deviation * jax.random.normal(own_key, dims, jnp.float32)
    if pieces:
        entries = entries * level_of(own_key, dims, pieces, -0.22, 0.18)
    return jnp.clip(entries, -bound, bound).astype(held_as)


def setup_inputs(seed: int = 0) -> dict:
    splits = jax.random.split(jax.random.key(seed), 9)
    return {
        "increment": scatter_about(splits[0], (LON, LAT, LEV), 1.0, 6.0, ((0, 8), (1, 4))),
        "jacobian": scatter_about(splits[1], (SCANS, NTAN, 3 * LON_DEV * BLEV), (BLAT * LON_DEV * BLEV) ** -0.5, 0.0625, ((0, 32),)),
        "lat_weight": jnp.clip(jnp.exp(math.log(2.0) - 2.3025851 * jax.random.uniform(splits[2], (SCANS, BLAT), jnp.float32) ** level_of(splits[2], (SCANS, BLAT), ((0, 32),), -0.2, 0.2)), 0.2, 2.0),
        "centre": place_ends(jax.random.randint(splits[3], (SCANS,), 0, LON_DEV), jax.random.fold_in(splits[3], 1), 0, LON_DEV - 1).astype(jnp.int32),
        "west": place_ends(jax.random.randint(splits[4], (SCANS,), 0, LON_DEV + 1), jax.random.fold_in(splits[4], 1), 0, LON_DEV).astype(jnp.int32),
        "east": place_ends(jax.random.randint(splits[5], (SCANS,), 0, LON_DEV + 1), jax.random.fold_in(splits[5], 1), 0, LON_DEV).astype(jnp.int32),
        "lat_offset": place_ends(jax.random.randint(splits[6], (SCANS,), 0, LAT - BLAT + 1), jax.random.fold_in(splits[6], 1), 0, LAT - BLAT).astype(jnp.int32),
        "lev_offset": place_ends(jax.random.randint(splits[7], (SCANS,), 0, LEV - BLEV + 1), jax.random.fold_in(splits[7], 1), 0, LEV - BLEV).astype(jnp.int32),
    }


def reference(increment, jacobian, lat_weight, centre, west, east, lat_offset, lev_offset):
    span = 3 * LON_DEV
    longitude = LON_DEV * N_LON

    def one_scan(item):
        index, kmat, weights, mid, left, right, lat_first, lev_first = item
        sector = index // (SLOTS * N_LAT)
        rows = jnp.arange(span, dtype=jnp.int32)
        columns = ((sector * LON_DEV - LON_DEV + rows) % longitude).astype(jnp.int32)
        window = jnp.take(increment, columns, axis=0)
        zero = jnp.zeros((), jnp.int32)
        box = lax.dynamic_slice(window, (zero, lat_first.astype(jnp.int32), lev_first.astype(jnp.int32)), (span, BLAT, BLEV))
        profile = jnp.einsum("rjk,j->rk", box.astype(jnp.float32), weights.astype(jnp.float32), precision=lax.Precision.HIGHEST)
        keep = (rows >= LON_DEV + mid - left) & (rows <= LON_DEV + mid + right)
        profile = jnp.where(keep[:, None], profile, jnp.zeros_like(profile)).astype(jnp.bfloat16)
        return jnp.dot(kmat, profile.reshape(-1), preferred_element_type=jnp.float32)

    indices = jnp.arange(SCANS, dtype=jnp.int32)
    return lax.map(one_scan, (indices, jacobian, lat_weight, centre, west, east, lat_offset, lev_offset))
```

```python
import functools

import jax
import jax.numpy as jnp
from jax import lax
from jax.experimental import pallas as pl
from jax.experimental.pallas import tpu as pltpu
from jax.sharding import PartitionSpec as P

BLAT = 8
BLEV = 32
HALO = 16
MESH = pl.DeviceIdType.MESH


def kernel(
    nlon, nlat, inc_ref, jac_ref, weight_ref, ints_ref, out_ref,
    ext, jbuf, info, sel, shift, pieces, recv,
    inc_sem, jac_sem, halo_send, halo_recv, info_send, info_recv, piece_send, piece_recv,
):
    lon = lax.axis_index("lon")
    lat = lax.axis_index("lat")
    width, rows, lev = inc_ref.shape
    slots, ntan = out_ref.shape
    group = lev // BLEV
    nq = width // group
    depth = rows + HALO
    listed = nlat * slots

    load = pltpu.make_async_copy(inc_ref, ext.at[:, pl.ds(0, rows), :], inc_sem)
    load.start()
    jload = pltpu.make_async_copy(jac_ref, jbuf, jac_sem)
    jload.start()

    def sector(t):
        return lax.rem(lon + t - 1 + nlon, nlon)

    peers = []
    for t in (0, 2, 1):
        for d in range(nlat):
            if t != 1 or d:
                peers.append((t, lax.rem(lat + d, nlat)))

    barrier = pltpu.get_barrier_semaphore()
    for t, l in peers:
        pl.semaphore_signal(barrier, inc=1, device_id=(sector(t), l), device_id_type=MESH)

    eye = lax.broadcasted_iota(jnp.int32, (slots, slots), 0) == lax.broadcasted_iota(
        jnp.int32, (slots, slots), 1
    )

    def column(i):
        row = jnp.broadcast_to(ints_ref[i : i + 1, :].astype(jnp.float32), (slots, slots))
        return jnp.sum(jnp.where(eye, row, 0.0), axis=1, keepdims=True)

    lane = lax.broadcasted_iota(jnp.int32, (slots, lev), 1)
    head = jnp.concatenate(
        [weight_ref[...], jnp.zeros((slots, lev - BLAT), jnp.float32)], axis=1
    )
    head = jnp.where(lane == BLAT, column(3), head)
    head = jnp.where(lane == BLAT + 1, column(4), head)
    info[1, lat] = head
    first = width + column(0) - column(1)
    last = width + column(0) + column(2)

    pl.semaphore_wait(barrier, len(peers))

    def info_copy(t, l):
        return pltpu.make_async_remote_copy(
            src_ref=info.at[1, lat], dst_ref=info.at[2 - t, lat],
            send_sem=info_send.at[t, l], recv_sem=info_recv.at[2 - t, lat],
            device_id=(sector(t), l), device_id_type=MESH,
        )

    for t, l in peers:
        info_copy(t, l).start()
    back = lax.rem(lat + nlat - 1, nlat)
    halo = pltpu.make_async_remote_copy(
        src_ref=inc_ref.at[:, pl.ds(0, HALO), :], dst_ref=ext.at[:, pl.ds(rows, HALO), :],
        send_sem=halo_send, recv_sem=halo_recv,
        device_id=(lon, back), device_id_type=MESH,
    )
    halo.start()

    def info_wait(t, l):
        pltpu.make_async_remote_copy(
            src_ref=info.at[1, lat], dst_ref=info.at[t, l],
            send_sem=info_send.at[t, l], recv_sem=info_recv.at[t, l],
            device_id=(sector(t), l), device_id_type=MESH,
        ).wait_recv()

    def piece_copy(t, l):
        return pltpu.make_async_remote_copy(
            src_ref=pieces.at[t, l], dst_ref=recv.at[2 - t, lat],
            send_sem=piece_send.at[t, l], recv_sem=piece_recv.at[2 - t, lat],
            device_id=(sector(t), l), device_id_type=MESH,
        )

    def piece_wait(t, l):
        pltpu.make_async_remote_copy(
            src_ref=pieces.at[t, l], dst_ref=recv.at[t, l],
            send_sem=piece_send.at[t, l], recv_sem=piece_recv.at[t, l],
            device_id=(sector(t), l), device_id_type=MESH,
        ).wait_recv()

    wide = lax.broadcasted_iota(jnp.int32, (listed, lev), 1)
    base = (lat * rows).astype(jnp.float32)

    ready = False
    for t in (0, 2, 1):
        for s, l in peers:
            if s == t:
                info_wait(t, l)
        table = info[t].reshape(listed, lev)
        local = table[:, BLAT : BLAT + 1] - base
        mine = (local >= 0.0) & (local < float(rows))
        start = jnp.broadcast_to(local, (listed, lev)).astype(jnp.int32)
        mine = jnp.broadcast_to(mine.astype(jnp.int32), (listed, lev)) > 0
        parts = []
        for begin in range(0, depth, lev):
            offset = wide + begin - start
            good = mine & (offset >= 0) & (offset < BLAT)
            picked = jnp.take_along_axis(table, jnp.clip(offset, 0, lev - 1), axis=1)
            parts.append(jnp.where(good, picked, 0.0))
        whole = jnp.concatenate(parts, axis=1)[:, :depth]
        high = whole.astype(jnp.bfloat16)
        low = (whole - high.astype(jnp.float32)).astype(jnp.bfloat16)
        sel[0:listed, :] = high
        sel[listed : 2 * listed, :] = low
        shift[...] = jnp.broadcast_to(table[:, BLAT + 1 : BLAT + 2], (listed, lev)).astype(
            jnp.int32
        ) + lax.rem(wide, BLEV)
        if not ready:
            load.wait()
            halo.wait_recv()
            ready = True

        @pl.loop(0, nq)
        def _(q):
            block = ext[pl.ds(q * group, group)]
            right = jnp.concatenate([block[g] for g in range(group)], axis=1)
            lifted = jnp.dot(sel[...], right, preferred_element_type=jnp.float32)
            lifted = lifted[:listed] + lifted[listed:]
            where = shift[...]
            total = jnp.zeros((listed, lev), jnp.float32)
            for g in range(group):
                moved = jnp.take_along_axis(lifted[:, g * lev : (g + 1) * lev], where, axis=1)
                inside = (wide >= g * BLEV) & (wide < (g + 1) * BLEV)
                total = jnp.where(inside, moved, total)
            total = total.astype(jnp.bfloat16)
            for l in range(nlat):
                pieces[t, l, q] = total[l * slots : (l + 1) * slots]

        for s, l in peers:
            if s == t:
                piece_copy(t, l).start()

    jload.wait()
    span = width * BLEV
    level_row = lax.broadcasted_iota(jnp.int32, (slots, span), 1) // BLEV
    which = lax.broadcasted_iota(jnp.int32, (slots, ntan), 0)
    answer = jnp.zeros((slots, ntan), jnp.float32)
    for t in (1, 0, 2):
        total = None
        if t == 1:
            total = pieces[1, lat].astype(jnp.float32)
        for s, l in peers:
            if s == t:
                piece_wait(t, l)
                value = recv[t, l].astype(jnp.float32)
                total = value if total is None else total + value
        flat = jnp.concatenate([total[q] for q in range(nq)], axis=1)
        at = (level_row + t * width).astype(jnp.float32)
        flat = jnp.where((at >= first) & (at <= last), flat, 0.0).astype(jnp.bfloat16)

        def step(i, answer):
            block = jbuf[pl.ds(2 * i, 2), :, pl.ds(t * span, span)].reshape(2 * ntan, span)
            both = lax.dot_general(
                flat, block, (((1,), (1,)), ((), ())), preferred_element_type=jnp.float32
            )
            answer = answer + jnp.where(which == 2 * i, both[:, :ntan], 0.0)
            return answer + jnp.where(which == 2 * i + 1, both[:, ntan:], 0.0)

        answer = lax.fori_loop(0, slots // 2, step, answer)
    out_ref[...] = answer

    halo.wait_send()
    for t, l in peers:
        info_copy(t, l).wait_send()
        piece_copy(t, l).wait_send()


def local(nlon, nlat, increment, jacobian, lat_weight, centre, west, east, lat_offset, lev_offset):
    width, rows, lev = increment.shape
    slots, ntan, span = jacobian.shape
    nq = width * BLEV // lev
    depth = rows + HALO
    ints = jnp.stack([centre, west, east, lat_offset, lev_offset])
    vmem = pl.BlockSpec(memory_space=pltpu.VMEM)
    hbm = pl.BlockSpec(memory_space=pl.ANY)
    dma = pltpu.SemaphoreType.DMA
    return pl.pallas_call(
        functools.partial(kernel, nlon, nlat),
        out_shape=jax.ShapeDtypeStruct((slots, ntan), jnp.float32),
        in_specs=[hbm, hbm, vmem, vmem],
        out_specs=vmem,
        scratch_shapes=[
            pltpu.VMEM((width, depth, lev), jnp.bfloat16),
            pltpu.VMEM((slots, ntan, span), jnp.bfloat16),
            pltpu.VMEM((3, nlat, slots, lev), jnp.float32),
            pltpu.VMEM((2 * nlat * slots, depth), jnp.bfloat16),
            pltpu.VMEM((nlat * slots, lev), jnp.int32),
            pltpu.VMEM((3, nlat, nq, slots, lev), jnp.bfloat16),
            pltpu.VMEM((3, nlat, nq, slots, lev), jnp.bfloat16),
            dma, dma, dma, dma,
            dma((3, nlat)), dma((3, nlat)), dma((3, nlat)), dma((3, nlat)),
        ],
        compiler_params=pltpu.CompilerParams(
            collective_id=0, has_side_effects=True, vmem_limit_bytes=48 << 20
        ),
    )(increment, jacobian, lat_weight, ints)


def solution(mesh):
    return jax.shard_map(
        functools.partial(local, mesh.shape["lon"], mesh.shape["lat"]),
        mesh=mesh,
        in_specs=(
            P("lon", "lat", None),
            P(("lon", "lat"), None, None),
            P(("lon", "lat"), None),
            P(("lon", "lat")),
            P(("lon", "lat")),
            P(("lon", "lat")),
            P(("lon", "lat")),
            P(("lon", "lat")),
        ),
        out_specs=P(("lon", "lat"), None),
        check_vma=False,
    )
```

```python
import functools

import jax
import jax.numpy as jnp
from jax import lax
from jax.experimental import pallas as pl
from jax.experimental.pallas import tpu as pltpu
from jax.sharding import PartitionSpec as P

BLAT = 8
BLEV = 32
HALO = 16
MESH = pl.DeviceIdType.MESH


def kernel(
    nlon, nlat, inc_ref, jac_ref, weight_ref, centre_ref, west_ref, east_ref, row_ref, level_ref,
    out_ref, ext, halo, jbuf, info, sel, pieces, recv,
    inc_sem, jac_sem, swap_send, swap_recv, halo_send, halo_recv,
    info_send, info_recv, piece_send, piece_recv,
):
    lon = lax.axis_index("lon")
    lat = lax.axis_index("lat")
    width, rows, lev = inc_ref.shape
    slots, ntan = out_ref.shape
    group = lev // BLEV
    nq = width // group
    part = nq // 2
    half = width // 2
    listed = nlat * slots
    pair = lat // 2
    side = lax.rem(lat, 2)
    npair = nlat // 2

    load = pltpu.make_async_copy(
        inc_ref.at[pl.ds(side * half, half)], ext.at[side], inc_sem
    )
    load.start()
    jload = pltpu.make_async_copy(jac_ref, jbuf, jac_sem)

    def sector(t):
        return lax.rem(lon + t - 1 + nlon, nlon)

    peers = []
    for t in (0, 2, 1):
        for d in range(nlat):
            if t != 1 or d:
                peers.append((t, lax.rem(lat + d, nlat)))

    barrier = pltpu.get_barrier_semaphore()
    for t, l in peers:
        pl.semaphore_signal(barrier, inc=1, device_id=(sector(t), l), device_id_type=MESH)
    jload.start()

    eye = lax.broadcasted_iota(jnp.int32, (slots, slots), 0) == lax.broadcasted_iota(
        jnp.int32, (slots, slots), 1
    )

    def column(row):
        row = jnp.broadcast_to(row.astype(jnp.float32), (slots, slots))
        return jnp.sum(jnp.where(eye, row, 0.0), axis=1, keepdims=True)

    lane = lax.broadcasted_iota(jnp.int32, (slots, lev), 1)
    head = jnp.zeros((slots, lev), jnp.float32)
    for j in range(BLAT):
        head = jnp.where(lane == j, column(weight_ref[j : j + 1, :]), head)
    head = jnp.where(lane == BLAT, column(row_ref[...]), head)
    head = jnp.where(lane == BLAT + 1, column(level_ref[...]), head)
    info[1, lat] = head
    middle = width + column(centre_ref[...])
    first = middle - column(west_ref[...])
    last = middle + column(east_ref[...])

    pl.semaphore_wait(barrier, len(peers))

    def info_copy(t, l):
        return pltpu.make_async_remote_copy(
            src_ref=info.at[1, lat], dst_ref=info.at[2 - t, lat],
            send_sem=info_send.at[t, l], recv_sem=info_recv.at[2 - t, lat],
            device_id=(sector(t), l), device_id_type=MESH,
        )

    for t, l in peers:
        info_copy(t, l).start()
    swap = pltpu.make_async_remote_copy(
        src_ref=inc_ref.at[pl.ds((1 - side) * half, half)], dst_ref=ext.at[side],
        send_sem=swap_send, recv_sem=swap_recv,
        device_id=(lon, pair * 2 + 1 - side), device_id_type=MESH,
    )

    def halo_copy(other):
        return pltpu.make_async_remote_copy(
            src_ref=inc_ref.at[pl.ds(other * half, half), pl.ds(0, HALO), :], dst_ref=halo,
            send_sem=halo_send.at[other], recv_sem=halo_recv,
            device_id=(lon, lax.rem(pair + npair - 1, npair) * 2 + other), device_id_type=MESH,
        )

    @pl.when(side == 0)
    def _():
        halo_copy(0).start()
        halo_copy(1).start()

    swap.start()

    def info_wait(t, l):
        pltpu.make_async_remote_copy(
            src_ref=info.at[1, lat], dst_ref=info.at[t, l],
            send_sem=info_send.at[t, l], recv_sem=info_recv.at[t, l],
            device_id=(sector(t), l), device_id_type=MESH,
        ).wait_recv()

    def slot(u, l):
        return recv.at[u, l // 2, pl.ds(lax.rem(l, 2) * part, part)]

    def piece_copy(t, l):
        return pltpu.make_async_remote_copy(
            src_ref=pieces.at[t, l], dst_ref=slot(2 - t, lat),
            send_sem=piece_send.at[t, l], recv_sem=piece_recv.at[2 - t, lat],
            device_id=(sector(t), l), device_id_type=MESH,
        )

    def piece_wait(t, l):
        pltpu.make_async_remote_copy(
            src_ref=pieces.at[t, l], dst_ref=slot(t, l),
            send_sem=piece_send.at[t, l], recv_sem=piece_recv.at[t, l],
            device_id=(sector(t), l), device_id_type=MESH,
        ).wait_recv()

    depth = 2 * rows + HALO
    wide = lax.broadcasted_iota(jnp.int32, (listed, lev), 1)
    base = (pair * 2 * rows).astype(jnp.float32)

    ready = False
    for t in (0, 2, 1):
        for s, l in peers:
            if s == t:
                info_wait(t, l)
        table = info[t].reshape(listed, lev)
        local = table[:, BLAT : BLAT + 1] - base
        mine = (local >= 0.0) & (local < float(2 * rows))
        start = jnp.broadcast_to(local, (listed, lev)).astype(jnp.int32)
        mine = jnp.broadcast_to(mine.astype(jnp.int32), (listed, lev)) > 0
        parts = []
        for begin in range(0, depth, lev):
            offset = wide + begin - start
            good = mine & (offset >= 0) & (offset < BLAT)
            picked = jnp.take_along_axis(table, jnp.clip(offset, 0, lev - 1), axis=1)
            parts.append(jnp.where(good, picked, 0.0))
        whole = jnp.concatenate(parts, axis=1)[:, :depth]
        high = whole.astype(jnp.bfloat16)
        low = (whole - high.astype(jnp.float32)).astype(jnp.bfloat16)
        sel[0:listed, :] = high
        sel[listed : 2 * listed, :] = low
        where = jnp.broadcast_to(table[:, BLAT + 1 : BLAT + 2], (listed, lev)).astype(
            jnp.int32
        ) + lax.rem(wide, BLEV)
        if not ready:
            load.wait()
            swap.wait_recv()
            halo_copy(0).wait_recv()
            ready = True

        for q in range(part):
            right = jnp.concatenate(
                [
                    jnp.concatenate(
                        [ext[0, q * group + g], ext[1, q * group + g], halo[q * group + g]], axis=0
                    )
                    for g in range(group)
                ],
                axis=1,
            )
            lifted = jnp.dot(sel[...], right, preferred_element_type=jnp.float32)
            lifted = lifted[:listed] + lifted[listed:]
            total = jnp.zeros((listed, lev), jnp.float32)
            for g in range(group):
                moved = jnp.take_along_axis(lifted[:, g * lev : (g + 1) * lev], where, axis=1)
                inside = (wide >= g * BLEV) & (wide < (g + 1) * BLEV)
                total = jnp.where(inside, moved, total)
            total = total.astype(jnp.bfloat16)
            for l in range(nlat):
                pieces[t, l, q] = total[l * slots : (l + 1) * slots]

        for s, l in peers:
            if s == t:
                piece_copy(t, l).start()

    keep = pltpu.make_async_copy(pieces.at[1, lat], slot(1, lat), inc_sem)
    keep.start()
    jload.wait()
    keep.wait()
    span = width * BLEV
    level_row = lax.broadcasted_iota(jnp.int32, (slots, span), 1) // BLEV
    which = lax.broadcasted_iota(jnp.int32, (slots, ntan), 0)
    answer = jnp.zeros((slots, ntan), jnp.float32)
    for t in (1, 0, 2):
        for s, l in peers:
            if s == t:
                piece_wait(t, l)
        total = recv[t, 0].astype(jnp.float32)
        for p in range(1, npair):
            total = total + recv[t, p].astype(jnp.float32)
        flat = jnp.concatenate([total[q] for q in range(nq)], axis=1)
        at = (level_row + t * width).astype(jnp.float32)
        flat = jnp.where((at >= first) & (at <= last), flat, 0.0).astype(jnp.bfloat16)

        def step(i, answer):
            block = jbuf[pl.ds(2 * i, 2), :, pl.ds(t * span, span)].reshape(2 * ntan, span)
            both = lax.dot_general(
                flat, block, (((1,), (1,)), ((), ())), preferred_element_type=jnp.float32
            )
            answer = answer + jnp.where(which == 2 * i, both[:, :ntan], 0.0)
            return answer + jnp.where(which == 2 * i + 1, both[:, ntan:], 0.0)

        answer = lax.fori_loop(0, slots // 2, step, answer)
    out_ref[...] = answer

    swap.wait_send()

    @pl.when(side == 0)
    def _():
        halo_copy(0).wait_send()
        halo_copy(1).wait_send()

    for t, l in peers:
        info_copy(t, l).wait_send()
        piece_copy(t, l).wait_send()


def local(nlon, nlat, increment, jacobian, lat_weight, centre, west, east, lat_offset, lev_offset):
    width, rows, lev = increment.shape
    slots, ntan, span = jacobian.shape
    nq = width * BLEV // lev
    vmem = pl.BlockSpec(memory_space=pltpu.VMEM)
    hbm = pl.BlockSpec(memory_space=pltpu.HBM)
    dma = pltpu.SemaphoreType.DMA
    ints = [v.reshape(1, slots) for v in (centre, west, east, lat_offset, lev_offset)]
    return pl.pallas_call(
        functools.partial(kernel, nlon, nlat),
        out_shape=jax.ShapeDtypeStruct((slots, ntan), jnp.float32),
        in_specs=[hbm, hbm] + [vmem] * 6,
        out_specs=vmem,
        scratch_shapes=[
            pltpu.VMEM((2, width // 2, rows, lev), jnp.bfloat16),
            pltpu.VMEM((width // 2, HALO, lev), jnp.bfloat16),
            pltpu.VMEM((slots, ntan, span), jnp.bfloat16),
            pltpu.VMEM((3, nlat, slots, lev), jnp.float32),
            pltpu.VMEM((2 * nlat * slots, 2 * rows + HALO), jnp.bfloat16),
            pltpu.VMEM((3, nlat, nq // 2, slots, lev), jnp.bfloat16),
            pltpu.VMEM((3, nlat // 2, nq, slots, lev), jnp.bfloat16),
            dma, dma, dma, dma, dma((2,)), dma,
            dma((3, nlat)), dma((3, nlat)), dma((3, nlat)), dma((3, nlat)),
        ],
        compiler_params=pltpu.CompilerParams(
            collective_id=0, has_side_effects=True, vmem_limit_bytes=56 << 20
        ),
    )(increment, jacobian, lat_weight.T, *ints)


def solution(mesh):
    return jax.shard_map(
        functools.partial(local, mesh.shape["lon"], mesh.shape["lat"]),
        mesh=mesh,
        in_specs=(
            P("lon", "lat", None),
            P(("lon", "lat"), None, None),
            P(("lon", "lat"), None),
            P(("lon", "lat")),
            P(("lon", "lat")),
            P(("lon", "lat")),
            P(("lon", "lat")),
            P(("lon", "lat")),
        ),
        out_specs=P(("lon", "lat"), None),
        check_vma=False,
    )
```

```python
import functools

import jax
import jax.numpy as jnp
from jax import lax
from jax.experimental import pallas as pl
from jax.experimental.pallas import tpu as pltpu
from jax.sharding import PartitionSpec as P

BLAT = 8
BLEV = 32
HALO = 8
FIELDS = 16
MESH = pl.DeviceIdType.MESH


def kernel(
    nlon, nlat, inc_ref, jac_ref, weight_ref, centre_ref, west_ref, east_ref, row_ref, level_ref,
    out_ref, ext, halo, jbuf, info, sel, pieces, recv,
    inc_sem, jac_sem, swap_send, swap_recv, halo_send, halo_recv,
    info_send, info_recv, piece_send, piece_recv,
):
    lon = lax.axis_index("lon")
    lat = lax.axis_index("lat")
    width, rows, lev = inc_ref.shape
    slots, ntan = out_ref.shape
    group = lev // BLEV
    nq = width // group
    part = nq // 2
    half = width // 2
    listed = nlat * slots
    packed = lev // FIELDS
    pair = lat // 2
    side = lax.rem(lat, 2)
    npair = nlat // 2

    load = pltpu.make_async_copy(
        inc_ref.at[pl.ds(side * half, half)], ext.at[side], inc_sem
    )
    load.start()
    jload = pltpu.make_async_copy(jac_ref, jbuf, jac_sem)

    def sector(t):
        return lax.rem(lon + t - 1 + nlon, nlon)

    peers = []
    for t in (0, 2, 1):
        for d in range(nlat):
            if t != 1 or d:
                peers.append((t, lax.rem(lat + d, nlat)))

    barrier = pltpu.get_barrier_semaphore()
    for t, l in peers:
        pl.semaphore_signal(barrier, inc=1, device_id=(sector(t), l), device_id_type=MESH)
    jload.start()

    eye = lax.broadcasted_iota(jnp.int32, (slots, slots), 0) == lax.broadcasted_iota(
        jnp.int32, (slots, slots), 1
    )

    def column(row):
        row = jnp.broadcast_to(row.astype(jnp.float32), (slots, slots))
        return jnp.sum(jnp.where(eye, row, 0.0), axis=1, keepdims=True)

    lane = lax.broadcasted_iota(jnp.int32, (slots, lev), 1)
    head = jnp.zeros((slots, lev), jnp.float32)
    for j in range(BLAT):
        head = jnp.where(lane == j, column(weight_ref[j : j + 1, :]), head)
    head = jnp.where(lane == BLAT, column(row_ref[...]), head)
    head = jnp.where(lane == BLAT + 1, column(level_ref[...]), head)
    place = lax.broadcasted_iota(jnp.int32, (slots, lev), 0)
    spread = jnp.take_along_axis(head, lax.rem(lane, FIELDS), axis=1)
    spread = jnp.where(lane // FIELDS == lax.rem(place, packed), spread, 0.0)
    info[1, lat] = jnp.concatenate(
        [
            jnp.sum(spread[r * packed : (r + 1) * packed], axis=0, keepdims=True)
            for r in range(slots // packed)
        ],
        axis=0,
    )
    middle = width + column(centre_ref[...])
    first = middle - column(west_ref[...])
    last = middle + column(east_ref[...])

    pl.semaphore_wait(barrier, len(peers))

    def info_copy(t, l):
        return pltpu.make_async_remote_copy(
            src_ref=info.at[1, lat], dst_ref=info.at[2 - t, lat],
            send_sem=info_send.at[t, l], recv_sem=info_recv.at[2 - t, lat],
            device_id=(sector(t), l), device_id_type=MESH,
        )

    for t, l in peers:
        info_copy(t, l).start()
    swap = pltpu.make_async_remote_copy(
        src_ref=inc_ref.at[pl.ds((1 - side) * half, half)], dst_ref=ext.at[side],
        send_sem=swap_send, recv_sem=swap_recv,
        device_id=(lon, pair * 2 + 1 - side), device_id_type=MESH,
    )

    def halo_copy(other):
        return pltpu.make_async_remote_copy(
            src_ref=inc_ref.at[pl.ds(other * half, half), pl.ds(0, HALO), :], dst_ref=halo,
            send_sem=halo_send.at[other], recv_sem=halo_recv,
            device_id=(lon, lax.rem(pair + npair - 1, npair) * 2 + other), device_id_type=MESH,
        )

    @pl.when(side == 0)
    def _():
        halo_copy(0).start()
        halo_copy(1).start()

    swap.start()

    def info_wait(t, l):
        pltpu.make_async_remote_copy(
            src_ref=info.at[1, lat], dst_ref=info.at[t, l],
            send_sem=info_send.at[t, l], recv_sem=info_recv.at[t, l],
            device_id=(sector(t), l), device_id_type=MESH,
        ).wait_recv()

    def slot(u, l):
        return recv.at[u, l // 2, pl.ds(lax.rem(l, 2) * part, part)]

    def piece_copy(t, l):
        return pltpu.make_async_remote_copy(
            src_ref=pieces.at[t, l], dst_ref=slot(2 - t, lat),
            send_sem=piece_send.at[t, l], recv_sem=piece_recv.at[2 - t, lat],
            device_id=(sector(t), l), device_id_type=MESH,
        )

    def piece_wait(t, l):
        pltpu.make_async_remote_copy(
            src_ref=pieces.at[t, l], dst_ref=slot(t, l),
            send_sem=piece_send.at[t, l], recv_sem=piece_recv.at[t, l],
            device_id=(sector(t), l), device_id_type=MESH,
        ).wait_recv()

    depth = 2 * rows + HALO
    wide = lax.broadcasted_iota(jnp.int32, (listed, lev), 1)
    unpack = lax.rem(
        lax.rem(lax.broadcasted_iota(jnp.int32, (listed, lev), 0), packed) * FIELDS + wide, lev
    )
    base = (pair * 2 * rows).astype(jnp.float32)

    ready = False
    for t in (1, 0, 2):
        for s, l in peers:
            if s == t:
                info_wait(t, l)
        table = jnp.concatenate(
            [
                jnp.broadcast_to(info[t, l, r : r + 1, :], (packed, lev))
                for l in range(nlat)
                for r in range(slots // packed)
            ],
            axis=0,
        )
        table = jnp.take_along_axis(table, unpack, axis=1)
        local = table[:, BLAT : BLAT + 1] - base
        mine = (local >= 0.0) & (local < float(2 * rows))
        start = jnp.broadcast_to(local, (listed, lev)).astype(jnp.int32)
        mine = jnp.broadcast_to(mine.astype(jnp.int32), (listed, lev)) > 0
        parts = []
        for begin in range(0, depth, lev):
            offset = wide + begin - start
            good = mine & (offset >= 0) & (offset < BLAT)
            picked = jnp.take_along_axis(table, jnp.clip(offset, 0, lev - 1), axis=1)
            parts.append(jnp.where(good, picked, 0.0))
        whole = jnp.concatenate(parts, axis=1)[:, :depth]
        high = whole.astype(jnp.bfloat16)
        low = (whole - high.astype(jnp.float32)).astype(jnp.bfloat16)
        sel[0:listed, :] = high
        sel[listed : 2 * listed, :] = low
        where = jnp.broadcast_to(table[:, BLAT + 1 : BLAT + 2], (listed, lev)).astype(
            jnp.int32
        ) + lax.rem(wide, BLEV)
        if not ready:
            load.wait()
            swap.wait_recv()
            halo_copy(0).wait_recv()
            ready = True

        for q in range(part):
            right = jnp.concatenate(
                [
                    jnp.concatenate(
                        [ext[0, q * group + g], ext[1, q * group + g], halo[q * group + g]], axis=0
                    )
                    for g in range(group)
                ],
                axis=1,
            )
            lifted = jnp.dot(sel[...], right, preferred_element_type=jnp.float32)
            lifted = lifted[:listed] + lifted[listed:]
            total = jnp.zeros((listed, lev), jnp.float32)
            for g in range(group):
                moved = jnp.take_along_axis(lifted[:, g * lev : (g + 1) * lev], where, axis=1)
                inside = (wide >= g * BLEV) & (wide < (g + 1) * BLEV)
                total = jnp.where(inside, moved, total)
            total = total.astype(jnp.bfloat16)
            for l in range(nlat):
                pieces[t, l, q] = total[l * slots : (l + 1) * slots]

        for s, l in peers:
            if s == t:
                piece_copy(t, l).start()

    keep = pltpu.make_async_copy(pieces.at[1, lat], slot(1, lat), inc_sem)
    keep.start()
    jload.wait()
    keep.wait()
    span = width * BLEV
    level_row = lax.broadcasted_iota(jnp.int32, (slots, span), 1) // BLEV
    which = lax.broadcasted_iota(jnp.int32, (slots, ntan), 0)
    answer = jnp.zeros((slots, ntan), jnp.float32)
    for t in (1, 2, 0):
        for s, l in peers:
            if s == t:
                piece_wait(t, l)
        total = recv[t, 0].astype(jnp.float32)
        for p in range(1, npair):
            total = total + recv[t, p].astype(jnp.float32)
        flat = jnp.concatenate([total[q] for q in range(nq)], axis=1)
        at = (level_row + t * width).astype(jnp.float32)
        flat = jnp.where((at >= first) & (at <= last), flat, 0.0).astype(jnp.bfloat16)

        for i in range(slots // 2):
            block = jbuf[2 * i : 2 * i + 2, :, t * span : (t + 1) * span].reshape(2 * ntan, span)
            both = lax.dot_general(
                flat, block, (((1,), (1,)), ((), ())), preferred_element_type=jnp.float32
            )
            answer = answer + jnp.where(which == 2 * i, both[:, :ntan], 0.0)
            answer = answer + jnp.where(which == 2 * i + 1, both[:, ntan:], 0.0)
    out_ref[...] = answer

    swap.wait_send()

    @pl.when(side == 0)
    def _():
        halo_copy(0).wait_send()
        halo_copy(1).wait_send()

    for t, l in peers:
        info_copy(t, l).wait_send()
        piece_copy(t, l).wait_send()


def local(nlon, nlat, increment, jacobian, lat_weight, centre, west, east, lat_offset, lev_offset):
    width, rows, lev = increment.shape
    slots, ntan, span = jacobian.shape
    nq = width * BLEV // lev
    vmem = pl.BlockSpec(memory_space=pltpu.VMEM)
    hbm = pl.BlockSpec(memory_space=pltpu.HBM)
    dma = pltpu.SemaphoreType.DMA
    ints = [v.reshape(1, slots) for v in (centre, west, east, lat_offset, lev_offset)]
    return pl.pallas_call(
        functools.partial(kernel, nlon, nlat),
        out_shape=jax.ShapeDtypeStruct((slots, ntan), jnp.float32),
        in_specs=[hbm, hbm] + [vmem] * 6,
        out_specs=vmem,
        scratch_shapes=[
            pltpu.VMEM((2, width // 2, rows, lev), jnp.bfloat16),
            pltpu.VMEM((width // 2, HALO, lev), jnp.bfloat16),
            pltpu.VMEM((slots, ntan, span), jnp.bfloat16),
            pltpu.VMEM((3, nlat, slots * FIELDS // lev, lev), jnp.float32),
            pltpu.VMEM((2 * nlat * slots, 2 * rows + HALO), jnp.bfloat16),
            pltpu.VMEM((3, nlat, nq // 2, slots, lev), jnp.bfloat16),
            pltpu.VMEM((3, nlat // 2, nq, slots, lev), jnp.bfloat16),
            dma, dma, dma, dma, dma((2,)), dma,
            dma((3, nlat)), dma((3, nlat)), dma((3, nlat)), dma((3, nlat)),
        ],
        compiler_params=pltpu.CompilerParams(
            collective_id=0, has_side_effects=True, vmem_limit_bytes=56 << 20
        ),
    )(increment, jacobian, lat_weight.T, *ints)


def solution(mesh):
    return jax.shard_map(
        functools.partial(local, mesh.shape["lon"], mesh.shape["lat"]),
        mesh=mesh,
        in_specs=(
            P("lon", "lat", None),
            P(("lon", "lat"), None, None),
            P(("lon", "lat"), None),
            P(("lon", "lat")),
            P(("lon", "lat")),
            P(("lon", "lat")),
            P(("lon", "lat")),
            P(("lon", "lat")),
        ),
        out_specs=P(("lon", "lat"), None),
        check_vma=False,
    )
```

```python
import functools

import jax
import jax.numpy as jnp
from jax import lax
from jax.experimental import pallas as pl
from jax.experimental.pallas import tpu as pltpu
from jax.sharding import PartitionSpec as P

BLAT = 8
BLEV = 32
HALO = 8
FIELDS = 16
MESH = pl.DeviceIdType.MESH


def kernel(
    nlon, nlat, inc_ref, jac_ref, weight_hbm, centre_hbm, west_hbm, east_hbm, row_hbm, level_hbm,
    out_ref, weight_ref, centre_ref, west_ref, east_ref, row_ref, level_ref, small_sem,
    ext, halo, jbuf, info, sel, pieces, recv,
    inc_sem, jac_sem, swap_send, swap_recv, halo_send, halo_recv,
    info_send, info_recv, piece_send, piece_recv,
):
    lon = lax.axis_index("lon")
    lat = lax.axis_index("lat")
    width, rows, lev = inc_ref.shape
    slots, ntan = out_ref.shape
    group = lev // BLEV
    nq = width // group
    part = nq // 2
    half = width // 2
    listed = nlat * slots
    packed = lev // FIELDS
    pair = lat // 2
    side = lax.rem(lat, 2)
    npair = nlat // 2

    load = pltpu.make_async_copy(
        inc_ref.at[pl.ds(side * half, half)], ext.at[side], inc_sem
    )
    jload = pltpu.make_async_copy(jac_ref, jbuf, jac_sem)

    def sector(t):
        return lax.rem(lon + t - 1 + nlon, nlon)

    peers = []
    for t in (0, 2, 1):
        for d in range(nlat):
            if t != 1 or d:
                peers.append((t, lax.rem(lat + d, nlat)))

    barrier = pltpu.get_barrier_semaphore()
    for t, l in peers:
        pl.semaphore_signal(barrier, inc=1, device_id=(sector(t), l), device_id_type=MESH)
    small = [
        pltpu.make_async_copy(source, target, small_sem.at[i])
        for i, (source, target) in enumerate(
            [
                (weight_hbm, weight_ref), (row_hbm, row_ref), (level_hbm, level_ref),
                (centre_hbm, centre_ref), (west_hbm, west_ref), (east_hbm, east_ref),
            ]
        )
    ]
    for copy in small:
        copy.start()
    load.start()
    jload.start()

    eye = lax.broadcasted_iota(jnp.int32, (slots, slots), 0) == lax.broadcasted_iota(
        jnp.int32, (slots, slots), 1
    )

    def column(row):
        row = jnp.broadcast_to(row.astype(jnp.float32), (slots, slots))
        return jnp.sum(jnp.where(eye, row, 0.0), axis=1, keepdims=True)

    for copy in small:
        copy.wait()
    lane = lax.broadcasted_iota(jnp.int32, (slots, lev), 1)
    head = jnp.zeros((slots, lev), jnp.float32)
    for j in range(BLAT):
        head = jnp.where(lane == j, column(weight_ref[j : j + 1, :]), head)
    head = jnp.where(lane == BLAT, column(row_ref[...]), head)
    head = jnp.where(lane == BLAT + 1, column(level_ref[...]), head)
    place = lax.broadcasted_iota(jnp.int32, (slots, lev), 0)
    spread = jnp.take_along_axis(head, lax.rem(lane, FIELDS), axis=1)
    spread = jnp.where(lane // FIELDS == lax.rem(place, packed), spread, 0.0)
    info[1, lat] = jnp.concatenate(
        [
            jnp.sum(spread[r * packed : (r + 1) * packed], axis=0, keepdims=True)
            for r in range(slots // packed)
        ],
        axis=0,
    )
    middle = width + column(centre_ref[...])
    first = middle - column(west_ref[...])
    last = middle + column(east_ref[...])

    pl.semaphore_wait(barrier, len(peers))

    def info_copy(t, l):
        return pltpu.make_async_remote_copy(
            src_ref=info.at[1, lat], dst_ref=info.at[2 - t, lat],
            send_sem=info_send.at[t, l], recv_sem=info_recv.at[2 - t, lat],
            device_id=(sector(t), l), device_id_type=MESH,
        )

    for t, l in peers:
        info_copy(t, l).start()
    swap = pltpu.make_async_remote_copy(
        src_ref=inc_ref.at[pl.ds((1 - side) * half, half)], dst_ref=ext.at[side],
        send_sem=swap_send, recv_sem=swap_recv,
        device_id=(lon, pair * 2 + 1 - side), device_id_type=MESH,
    )

    def halo_copy(other):
        return pltpu.make_async_remote_copy(
            src_ref=inc_ref.at[pl.ds(other * half, half), pl.ds(0, HALO), :], dst_ref=halo,
            send_sem=halo_send.at[other], recv_sem=halo_recv,
            device_id=(lon, lax.rem(pair + npair - 1, npair) * 2 + other), device_id_type=MESH,
        )

    @pl.when(side == 0)
    def _():
        halo_copy(0).start()
        halo_copy(1).start()

    swap.start()

    def info_wait(t, l):
        pltpu.make_async_remote_copy(
            src_ref=info.at[1, lat], dst_ref=info.at[t, l],
            send_sem=info_send.at[t, l], recv_sem=info_recv.at[t, l],
            device_id=(sector(t), l), device_id_type=MESH,
        ).wait_recv()

    def slot(u, l):
        return recv.at[u, l // 2, pl.ds(lax.rem(l, 2) * part, part)]

    def piece_copy(t, l):
        return pltpu.make_async_remote_copy(
            src_ref=pieces.at[t, l], dst_ref=slot(2 - t, lat),
            send_sem=piece_send.at[t, l], recv_sem=piece_recv.at[2 - t, lat],
            device_id=(sector(t), l), device_id_type=MESH,
        )

    def piece_wait(t, l):
        pltpu.make_async_remote_copy(
            src_ref=pieces.at[t, l], dst_ref=slot(t, l),
            send_sem=piece_send.at[t, l], recv_sem=piece_recv.at[t, l],
            device_id=(sector(t), l), device_id_type=MESH,
        ).wait_recv()

    depth = 2 * rows + HALO
    wide = lax.broadcasted_iota(jnp.int32, (listed, lev), 1)
    unpack = lax.rem(
        lax.rem(lax.broadcasted_iota(jnp.int32, (listed, lev), 0), packed) * FIELDS + wide, lev
    )
    base = (pair * 2 * rows).astype(jnp.float32)

    ready = False
    for t in (1, 0, 2):
        for s, l in peers:
            if s == t:
                info_wait(t, l)
        table = jnp.concatenate(
            [
                jnp.broadcast_to(info[t, l, r : r + 1, :], (packed, lev))
                for l in range(nlat)
                for r in range(slots // packed)
            ],
            axis=0,
        )
        table = jnp.take_along_axis(table, unpack, axis=1)
        local = table[:, BLAT : BLAT + 1] - base
        mine = (local >= 0.0) & (local < float(2 * rows))
        start = jnp.broadcast_to(local, (listed, lev)).astype(jnp.int32)
        mine = jnp.broadcast_to(mine.astype(jnp.int32), (listed, lev)) > 0
        parts = []
        for begin in range(0, depth, lev):
            offset = wide + begin - start
            good = mine & (offset >= 0) & (offset < BLAT)
            picked = jnp.take_along_axis(table, jnp.clip(offset, 0, lev - 1), axis=1)
            parts.append(jnp.where(good, picked, 0.0))
        whole = jnp.concatenate(parts, axis=1)[:, :depth]
        high = whole.astype(jnp.bfloat16)
        low = (whole - high.astype(jnp.float32)).astype(jnp.bfloat16)
        sel[0:listed, :] = high
        sel[listed : 2 * listed, :] = low
        where = jnp.broadcast_to(table[:, BLAT + 1 : BLAT + 2], (listed, lev)).astype(
            jnp.int32
        ) + lax.rem(wide, BLEV)
        if not ready:
            load.wait()
            swap.wait_recv()
            halo_copy(0).wait_recv()
            ready = True

        for q in range(part):
            right = jnp.concatenate(
                [
                    jnp.concatenate(
                        [ext[0, q * group + g], ext[1, q * group + g], halo[q * group + g]], axis=0
                    )
                    for g in range(group)
                ],
                axis=1,
            )
            lifted = jnp.dot(sel[...], right, preferred_element_type=jnp.float32)
            lifted = lifted[:listed] + lifted[listed:]
            total = jnp.zeros((listed, lev), jnp.float32)
            for g in range(group):
                moved = jnp.take_along_axis(lifted[:, g * lev : (g + 1) * lev], where, axis=1)
                inside = (wide >= g * BLEV) & (wide < (g + 1) * BLEV)
                total = jnp.where(inside, moved, total)
            total = total.astype(jnp.bfloat16)
            for l in range(nlat):
                pieces[t, l, q] = total[l * slots : (l + 1) * slots]

        for s, l in peers:
            if s == t:
                piece_copy(t, l).start()

    keep = pltpu.make_async_copy(pieces.at[1, lat], slot(1, lat), inc_sem)
    keep.start()
    jload.wait()
    keep.wait()
    span = width * BLEV
    level_row = lax.broadcasted_iota(jnp.int32, (slots, span), 1) // BLEV
    which = lax.broadcasted_iota(jnp.int32, (slots, ntan), 0)
    answer = jnp.zeros((slots, ntan), jnp.float32)
    for t in (1, 2, 0):
        for s, l in peers:
            if s == t:
                piece_wait(t, l)
        total = recv[t, 0].astype(jnp.float32)
        for p in range(1, npair):
            total = total + recv[t, p].astype(jnp.float32)
        flat = jnp.concatenate([total[q] for q in range(nq)], axis=1)
        at = (level_row + t * width).astype(jnp.float32)
        flat = jnp.where((at >= first) & (at <= last), flat, 0.0).astype(jnp.bfloat16)

        for i in range(slots // 2):
            block = jbuf[2 * i : 2 * i + 2, :, t * span : (t + 1) * span].reshape(2 * ntan, span)
            both = lax.dot_general(
                flat, block, (((1,), (1,)), ((), ())), preferred_element_type=jnp.float32
            )
            answer = answer + jnp.where(which == 2 * i, both[:, :ntan], 0.0)
            answer = answer + jnp.where(which == 2 * i + 1, both[:, ntan:], 0.0)
    out_ref[...] = answer

    swap.wait_send()

    @pl.when(side == 0)
    def _():
        halo_copy(0).wait_send()
        halo_copy(1).wait_send()

    for t, l in peers:
        info_copy(t, l).wait_send()
        piece_copy(t, l).wait_send()


def local(nlon, nlat, increment, jacobian, lat_weight, centre, west, east, lat_offset, lev_offset):
    width, rows, lev = increment.shape
    slots, ntan, span = jacobian.shape
    nq = width * BLEV // lev
    vmem = pl.BlockSpec(memory_space=pltpu.VMEM)
    hbm = pl.BlockSpec(memory_space=pltpu.HBM)
    dma = pltpu.SemaphoreType.DMA
    ints = [v.reshape(1, slots) for v in (centre, west, east, lat_offset, lev_offset)]
    return pl.pallas_call(
        functools.partial(kernel, nlon, nlat),
        out_shape=pltpu.VMEM((slots, ntan), jnp.float32),
        in_specs=[hbm] * 8,
        out_specs=vmem,
        scratch_shapes=[
            pltpu.VMEM((BLAT, slots), jnp.float32),
            *[pltpu.VMEM((1, slots), jnp.int32)] * 5,
            dma((6,)),
            pltpu.VMEM((2, width // 2, rows, lev), jnp.bfloat16),
            pltpu.VMEM((width // 2, HALO, lev), jnp.bfloat16),
            pltpu.VMEM((slots, ntan, span), jnp.bfloat16),
            pltpu.VMEM((3, nlat, slots * FIELDS // lev, lev), jnp.float32),
            pltpu.VMEM((2 * nlat * slots, 2 * rows + HALO), jnp.bfloat16),
            pltpu.VMEM((3, nlat, nq // 2, slots, lev), jnp.bfloat16),
            pltpu.VMEM((3, nlat // 2, nq, slots, lev), jnp.bfloat16),
            dma, dma, dma, dma, dma((2,)), dma,
            dma((3, nlat)), dma((3, nlat)), dma((3, nlat)), dma((3, nlat)),
        ],
        compiler_params=pltpu.CompilerParams(
            collective_id=0, has_side_effects=True, vmem_limit_bytes=56 << 20
        ),
    )(increment, jacobian, lat_weight.T, *ints)


def solution(mesh):
    return jax.shard_map(
        functools.partial(local, mesh.shape["lon"], mesh.shape["lat"]),
        mesh=mesh,
        in_specs=(
            P("lon", "lat", None),
            P(("lon", "lat"), None, None),
            P(("lon", "lat"), None),
            P(("lon", "lat")),
            P(("lon", "lat")),
            P(("lon", "lat")),
            P(("lon", "lat")),
            P(("lon", "lat")),
        ),
        out_specs=P(("lon", "lat"), None),
        check_vma=False,
    )
```

```python
import functools

import jax
import jax.numpy as jnp
from jax import lax
from jax.experimental import pallas as pl
from jax.experimental.pallas import tpu as pltpu
from jax.sharding import PartitionSpec as P

BLAT = 8
BLEV = 32
HALO = 8
FIELDS = 16
MESH = pl.DeviceIdType.MESH


def kernel(
    nlon, nlat, inc_ref, jac_ref, weight_hbm, centre_hbm, west_hbm, east_hbm, row_hbm, level_hbm,
    out_ref, weight_ref, centre_ref, west_ref, east_ref, row_ref, level_ref, small_sem,
    ext, halo, jbuf, info, sel, pieces, recv,
    inc_sem, jac_sem, swap_send, swap_recv, halo_send, halo_recv,
    info_send, info_recv, piece_send, piece_recv,
):
    lon = lax.axis_index("lon")
    lat = lax.axis_index("lat")
    width, rows, lev = inc_ref.shape
    slots, ntan = out_ref.shape
    group = lev // BLEV
    nq = width // group
    part = nq // 2
    half = width // 2
    listed = nlat * slots
    packed = lev // FIELDS
    pair = lat // 2
    side = lax.rem(lat, 2)
    npair = nlat // 2

    load = pltpu.make_async_copy(
        inc_ref.at[pl.ds(side * half, half)], ext.at[side], inc_sem
    )
    jload = pltpu.make_async_copy(jac_ref, jbuf, jac_sem)

    def sector(t):
        return lax.rem(lon + t - 1 + nlon, nlon)

    peers = []
    for t in (0, 2, 1):
        for d in range(nlat):
            if t != 1 or d:
                peers.append((t, lax.rem(lat + d, nlat)))

    barrier = pltpu.get_barrier_semaphore()
    for t, l in peers:
        pl.semaphore_signal(barrier, inc=1, device_id=(sector(t), l), device_id_type=MESH)
    small = [
        pltpu.make_async_copy(source, target, small_sem.at[i])
        for i, (source, target) in enumerate(
            [
                (weight_hbm, weight_ref), (row_hbm, row_ref), (level_hbm, level_ref),
                (centre_hbm, centre_ref), (west_hbm, west_ref), (east_hbm, east_ref),
            ]
        )
    ]
    for copy in small:
        copy.start()
    load.start()
    jload.start()

    eye = lax.broadcasted_iota(jnp.int32, (slots, slots), 0) == lax.broadcasted_iota(
        jnp.int32, (slots, slots), 1
    )

    def column(row):
        row = jnp.broadcast_to(row.astype(jnp.float32), (slots, slots))
        return jnp.sum(jnp.where(eye, row, 0.0), axis=1, keepdims=True)

    for copy in small[:3]:
        copy.wait()
    lane = lax.broadcasted_iota(jnp.int32, (slots, lev), 1)
    head = jnp.zeros((slots, lev), jnp.float32)
    for j in range(BLAT):
        head = jnp.where(lane == j, column(weight_ref[j : j + 1, :]), head)
    head = jnp.where(lane == BLAT, column(row_ref[...]), head)
    head = jnp.where(lane == BLAT + 1, column(level_ref[...]), head)
    place = lax.broadcasted_iota(jnp.int32, (slots, lev), 0)
    spread = jnp.take_along_axis(head, lax.rem(lane, FIELDS), axis=1)
    spread = jnp.where(lane // FIELDS == lax.rem(place, packed), spread, 0.0)
    info[1, lat] = jnp.concatenate(
        [
            jnp.sum(spread[r * packed : (r + 1) * packed], axis=0, keepdims=True)
            for r in range(slots // packed)
        ],
        axis=0,
    )

    pl.semaphore_wait(barrier, len(peers))

    def info_copy(t, l):
        return pltpu.make_async_remote_copy(
            src_ref=info.at[1, lat], dst_ref=info.at[2 - t, lat],
            send_sem=info_send.at[t, l], recv_sem=info_recv.at[2 - t, lat],
            device_id=(sector(t), l), device_id_type=MESH,
        )

    for t, l in peers:
        info_copy(t, l).start()
    swap = pltpu.make_async_remote_copy(
        src_ref=inc_ref.at[pl.ds((1 - side) * half, half)], dst_ref=ext.at[side],
        send_sem=swap_send, recv_sem=swap_recv,
        device_id=(lon, pair * 2 + 1 - side), device_id_type=MESH,
    )

    def halo_copy(other):
        return pltpu.make_async_remote_copy(
            src_ref=inc_ref.at[pl.ds(other * half, half), pl.ds(0, HALO), :], dst_ref=halo,
            send_sem=halo_send.at[other], recv_sem=halo_recv,
            device_id=(lon, lax.rem(pair + npair - 1, npair) * 2 + other), device_id_type=MESH,
        )

    @pl.when(side == 0)
    def _():
        halo_copy(0).start()
        halo_copy(1).start()

    swap.start()
    for copy in small[3:]:
        copy.wait()
    middle = width + column(centre_ref[...])
    first = middle - column(west_ref[...])
    last = middle + column(east_ref[...])

    def info_wait(t, l):
        pltpu.make_async_remote_copy(
            src_ref=info.at[1, lat], dst_ref=info.at[t, l],
            send_sem=info_send.at[t, l], recv_sem=info_recv.at[t, l],
            device_id=(sector(t), l), device_id_type=MESH,
        ).wait_recv()

    def slot(u, l):
        return recv.at[u, l // 2, pl.ds(lax.rem(l, 2) * part, part)]

    def piece_copy(t, l):
        return pltpu.make_async_remote_copy(
            src_ref=pieces.at[t, l], dst_ref=slot(2 - t, lat),
            send_sem=piece_send.at[t, l], recv_sem=piece_recv.at[2 - t, lat],
            device_id=(sector(t), l), device_id_type=MESH,
        )

    def piece_wait(t, l):
        pltpu.make_async_remote_copy(
            src_ref=pieces.at[t, l], dst_ref=slot(t, l),
            send_sem=piece_send.at[t, l], recv_sem=piece_recv.at[t, l],
            device_id=(sector(t), l), device_id_type=MESH,
        ).wait_recv()

    depth = 2 * rows + HALO
    wide = lax.broadcasted_iota(jnp.int32, (listed, lev), 1)
    unpack = lax.rem(
        lax.rem(lax.broadcasted_iota(jnp.int32, (listed, lev), 0), packed) * FIELDS + wide, lev
    )
    base = (pair * 2 * rows).astype(jnp.float32)

    ready = False
    for t in (1, 0, 2):
        for s, l in peers:
            if s == t:
                info_wait(t, l)
        table = jnp.concatenate(
            [
                jnp.broadcast_to(info[t, l, r : r + 1, :], (packed, lev))
                for l in range(nlat)
                for r in range(slots // packed)
            ],
            axis=0,
        )
        table = jnp.take_along_axis(table, unpack, axis=1)
        local = table[:, BLAT : BLAT + 1] - base
        mine = (local >= 0.0) & (local < float(2 * rows))
        start = jnp.broadcast_to(local, (listed, lev)).astype(jnp.int32)
        mine = jnp.broadcast_to(mine.astype(jnp.int32), (listed, lev)) > 0
        parts = []
        for begin in range(0, depth, lev):
            offset = wide + begin - start
            good = mine & (offset >= 0) & (offset < BLAT)
            picked = jnp.take_along_axis(table, jnp.clip(offset, 0, lev - 1), axis=1)
            parts.append(jnp.where(good, picked, 0.0))
        whole = jnp.concatenate(parts, axis=1)[:, :depth]
        high = whole.astype(jnp.bfloat16)
        low = (whole - high.astype(jnp.float32)).astype(jnp.bfloat16)
        sel[0:listed, :] = high
        sel[listed : 2 * listed, :] = low
        where = jnp.broadcast_to(table[:, BLAT + 1 : BLAT + 2], (listed, lev)).astype(
            jnp.int32
        ) + lax.rem(wide, BLEV)
        if not ready:
            load.wait()
            swap.wait_recv()
            halo_copy(0).wait_recv()
            ready = True

        for q in range(part):
            right = jnp.concatenate(
                [
                    jnp.concatenate(
                        [ext[0, q * group + g], ext[1, q * group + g], halo[q * group + g]], axis=0
                    )
                    for g in range(group)
                ],
                axis=1,
            )
            lifted = jnp.dot(sel[...], right, preferred_element_type=jnp.float32)
            lifted = lifted[:listed] + lifted[listed:]
            total = jnp.zeros((listed, lev), jnp.float32)
            for g in range(group):
                moved = jnp.take_along_axis(lifted[:, g * lev : (g + 1) * lev], where, axis=1)
                inside = (wide >= g * BLEV) & (wide < (g + 1) * BLEV)
                total = jnp.where(inside, moved, total)
            total = total.astype(jnp.bfloat16)
            for l in range(nlat):
                pieces[t, l, q] = total[l * slots : (l + 1) * slots]

        for s, l in peers:
            if s == t:
                piece_copy(t, l).start()

    keep = pltpu.make_async_copy(pieces.at[1, lat], slot(1, lat), inc_sem)
    keep.start()
    jload.wait()
    keep.wait()
    span = width * BLEV
    level_row = lax.broadcasted_iota(jnp.int32, (slots, span), 1) // BLEV
    which = lax.broadcasted_iota(jnp.int32, (slots, ntan), 0)
    answer = jnp.zeros((slots, ntan), jnp.float32)
    for t in (1, 2, 0):
        for s, l in peers:
            if s == t:
                piece_wait(t, l)
        total = recv[t, 0].astype(jnp.float32)
        for p in range(1, npair):
            total = total + recv[t, p].astype(jnp.float32)
        flat = jnp.concatenate([total[q] for q in range(nq)], axis=1)
        at = (level_row + t * width).astype(jnp.float32)
        flat = jnp.where((at >= first) & (at <= last), flat, 0.0).astype(jnp.bfloat16)

        for i in range(slots // 2):
            block = jbuf[2 * i : 2 * i + 2, :, t * span : (t + 1) * span].reshape(2 * ntan, span)
            both = lax.dot_general(
                flat, block, (((1,), (1,)), ((), ())), preferred_element_type=jnp.float32
            )
            answer = answer + jnp.where(which == 2 * i, both[:, :ntan], 0.0)
            answer = answer + jnp.where(which == 2 * i + 1, both[:, ntan:], 0.0)
    out_ref[...] = answer

    swap.wait_send()

    @pl.when(side == 0)
    def _():
        halo_copy(0).wait_send()
        halo_copy(1).wait_send()

    for t, l in peers:
        info_copy(t, l).wait_send()
        piece_copy(t, l).wait_send()


def local(nlon, nlat, increment, jacobian, lat_weight, centre, west, east, lat_offset, lev_offset):
    width, rows, lev = increment.shape
    slots, ntan, span = jacobian.shape
    nq = width * BLEV // lev
    vmem = pl.BlockSpec(memory_space=pltpu.VMEM)
    hbm = pl.BlockSpec(memory_space=pltpu.HBM)
    dma = pltpu.SemaphoreType.DMA
    ints = [v.reshape(1, slots) for v in (centre, west, east, lat_offset, lev_offset)]
    return pl.pallas_call(
        functools.partial(kernel, nlon, nlat),
        out_shape=pltpu.VMEM((slots, ntan), jnp.float32),
        in_specs=[hbm] * 8,
        out_specs=vmem,
        scratch_shapes=[
            pltpu.VMEM((BLAT, slots), jnp.float32),
            *[pltpu.VMEM((1, slots), jnp.int32)] * 5,
            dma((6,)),
            pltpu.VMEM((2, width // 2, rows, lev), jnp.bfloat16),
            pltpu.VMEM((width // 2, HALO, lev), jnp.bfloat16),
            pltpu.VMEM((slots, ntan, span), jnp.bfloat16),
            pltpu.VMEM((3, nlat, slots * FIELDS // lev, lev), jnp.float32),
            pltpu.VMEM((2 * nlat * slots, 2 * rows + HALO), jnp.bfloat16),
            pltpu.VMEM((3, nlat, nq // 2, slots, lev), jnp.bfloat16),
            pltpu.VMEM((3, nlat // 2, nq, slots, lev), jnp.bfloat16),
            dma, dma, dma, dma, dma((2,)), dma,
            dma((3, nlat)), dma((3, nlat)), dma((3, nlat)), dma((3, nlat)),
        ],
        compiler_params=pltpu.CompilerParams(
            collective_id=0, has_side_effects=True, vmem_limit_bytes=56 << 20
        ),
    )(increment, jacobian, lat_weight.T, *ints)


def solution(mesh):
    return jax.shard_map(
        functools.partial(local, mesh.shape["lon"], mesh.shape["lat"]),
        mesh=mesh,
        in_specs=(
            P("lon", "lat", None),
            P(("lon", "lat"), None, None),
            P(("lon", "lat"), None),
            P(("lon", "lat")),
            P(("lon", "lat")),
            P(("lon", "lat")),
            P(("lon", "lat")),
            P(("lon", "lat")),
        ),
        out_specs=P(("lon", "lat"), None),
        check_vma=False,
    )
```
